32 devices in a mesh: tm: 4 (over y, core), feed: 8 (over z, x).
Axes of the slice: x: 2, y: 2, z: 4, core: 2. Of those that a mesh axis runs over, the one named last changes fastest.
Arguments:
- voltages: bfloat16 [12, 1024, 16384], P('tm', 'feed'), may hold values from -6 to 6
- pfb_taps: float32 [4, 16384], replicated, may hold values from 0.2 to 1
- feed_of_slot: int32 [1024], replicated, may hold values from 0 to 1023, each once
Outputs:
- beam_power: float32 [4, 1024, 8192], P('tm', None, 'feed')
The draws below stay inside these ranges and needn't reach their ends.
Inputs may be any that keep to these rules, and one draw needn't show every extreme that they name: feed_of_slot[256 * r + j] is the feed at position j of cylinder r; every feed stands at exactly one position.
All inputs are finite; a program needn't handle non-finite values.
Results may differ from the reference program's by a relative error of at most 0.0052.
Values may be sent and summed in bfloat16 or wider, within the bound.
No kernel may reach another device: no remote copies, remote signals or barrier semaphores. Data moves between devices by JAX's collectives and lax.ppermute only.
A program may use at most 128 MiB of HBM per device.

```python
import math
import jax
import jax.numpy as jnp
from jax import lax

CYLINDERS = 4
COL_FEEDS = 256
SECTION_ONE = 128
SECTION_TWO = 128
FIR_TAPS = 4
SPECTRA_DEV = 3
FEED_COUNT = 1024
BEAM_COUNT = 1024
BLOCK_LEN = 16384
CHANNELS = 8192
SPECTRA = 12
N_TM = 4


def level_of(key, dims, pieces, smallest, top_value):
    level = 1.0
    for axis_at, blocks in pieces:
        steps = jax.random.uniform(jax.random.fold_in(jax.random.fold_in(key, 6), axis_at), (blocks,), jnp.float32, smallest / len(pieces), top_value / len(pieces))
        level = level * jnp.repeat(jnp.exp(steps), dims[axis_at] // blocks).reshape((-1,) + (1,) * (len(dims) - 1 - axis_at))
    return level


def normal_values(key, shape, scale, reach, split=(), kind=jnp.bfloat16):
    factor_of = level_of(key, shape, split, -0.22, 0.18) if split else 1.0
    array = jax.random.normal(key, shape, jnp.float32) * scale * factor_of
    return jnp.minimum(jnp.maximum(array, -reach), reach).astype(kind)


def setup_inputs(seed: int = 0) -> dict:
    key_list = jax.random.split(jax.random.key(seed), 4)
    return {
        "voltages": normal_values(key_list[0], (SPECTRA, FEED_COUNT, BLOCK_LEN), 1.0, 6.0, ((0, 4), (1, 8))),
        "pfb_taps": jnp.clip(jax.random.uniform(key_list[1], (FIR_TAPS, BLOCK_LEN), jnp.float32, 0.2, 1.0), 0.2, 1.0),
        "feed_of_slot": jax.random.permutation(key_list[2], FEED_COUNT).astype(jnp.int32),
    }


def tables(columns, row_count, period, factor):
    row_index = jnp.arange(row_count, dtype=jnp.int32)[:, None]
    col_index = jnp.arange(columns, dtype=jnp.int32)[None, :]
    angles = (row_index * col_index % period).astype(jnp.float32) * (2.0 * math.pi / period)
    return (jnp.cos(angles) * factor, -jnp.sin(angles) * factor)

def rounded(table):
    return table.astype(jnp.bfloat16).astype(jnp.float32)

def channelize(filtered):
    framed = filtered.reshape(FEED_COUNT, SECTION_ONE, SECTION_TWO).astype(jnp.float32)
    one_re, one_im = tables(SECTION_ONE, SECTION_ONE, SECTION_ONE, 1.0)
    one_re, one_im = (rounded(one_re), rounded(one_im))
    hp = lax.Precision.HIGHEST
    first_re = jnp.einsum('kn,fnm->fkm', one_re, framed, precision=hp)
    first_im = jnp.einsum('kn,fnm->fkm', one_im, framed, precision=hp)
    twist_re, twist_im = tables(SECTION_TWO, SECTION_ONE, BLOCK_LEN, 1.0)
    factor = 1.0 / math.sqrt(BLOCK_LEN)
    turned_re = ((first_re * twist_re - first_im * twist_im) * factor).astype(jnp.bfloat16).astype(jnp.float32)
    turned_im = ((first_re * twist_im + first_im * twist_re) * factor).astype(jnp.bfloat16).astype(jnp.float32)
    two_re, two_im = tables(SECTION_TWO, SECTION_TWO // 2, SECTION_TWO, 1.0)
    two_re, two_im = (rounded(two_re), rounded(two_im))
    spec_re = jnp.einsum('qm,fkm->fqk', two_re, turned_re, precision=hp) - jnp.einsum('qm,fkm->fqk', two_im, turned_im, precision=hp)
    spec_im = jnp.einsum('qm,fkm->fqk', two_re, turned_im, precision=hp) + jnp.einsum('qm,fkm->fqk', two_im, turned_re, precision=hp)
    return (spec_re.astype(jnp.bfloat16), spec_im.astype(jnp.bfloat16))

def power_of(spec_re, spec_im, feed_of_slot):
    hp = lax.Precision.HIGHEST
    shape = (CYLINDERS, COL_FEEDS, spec_re.shape[1], spec_re.shape[2])
    grid_re = jnp.take(spec_re, feed_of_slot, axis=0).reshape(shape).astype(jnp.float32)
    grid_im = jnp.take(spec_im, feed_of_slot, axis=0).reshape(shape).astype(jnp.float32)
    col_re, col_im = tables(COL_FEEDS, COL_FEEDS, COL_FEEDS, 1.0 / math.sqrt(COL_FEEDS))
    col_re, col_im = (rounded(col_re), rounded(col_im))
    along_re = jnp.einsum('jf,cfqk->cjqk', col_re, grid_re, precision=hp) - jnp.einsum('jf,cfqk->cjqk', col_im, grid_im, precision=hp)
    along_im = jnp.einsum('jf,cfqk->cjqk', col_re, grid_im, precision=hp) + jnp.einsum('jf,cfqk->cjqk', col_im, grid_re, precision=hp)
    cyl_re, cyl_im = tables(CYLINDERS, CYLINDERS, CYLINDERS, 1.0 / math.sqrt(CYLINDERS))
    beam_re = jnp.einsum('mc,cjqk->mjqk', cyl_re, along_re, precision=hp) - jnp.einsum('mc,cjqk->mjqk', cyl_im, along_im, precision=hp)
    beam_im = jnp.einsum('mc,cjqk->mjqk', cyl_re, along_im, precision=hp) + jnp.einsum('mc,cjqk->mjqk', cyl_im, along_re, precision=hp)
    return (beam_re * beam_re + beam_im * beam_im).reshape(BEAM_COUNT, CHANNELS)

def reference(voltages, pfb_taps, feed_of_slot):

    def one_block(time_block):

        def add_spectrum(position, running):
            spectrum = (time_block * SPECTRA_DEV + position).astype(jnp.int32)
            filtered = jnp.zeros((FEED_COUNT, BLOCK_LEN), jnp.float32)
            for tap_index in range(FIR_TAPS):
                source = (spectrum + tap_index).astype(jnp.int32)
                inside = jnp.where(source < SPECTRA, 1.0, 0.0).astype(jnp.float32)
                clamped = jnp.minimum(source, SPECTRA - 1).astype(jnp.int32)
                voltage_block = lax.dynamic_index_in_dim(voltages, clamped, 0, keepdims=False)
                filtered = filtered + pfb_taps[tap_index][None, :] * (voltage_block.astype(jnp.float32) * inside)
            spec_re, spec_im = channelize(filtered.astype(jnp.bfloat16))
            return running + power_of(spec_re, spec_im, feed_of_slot)
        return lax.fori_loop(0, SPECTRA_DEV, add_spectrum, jnp.zeros((BEAM_COUNT, CHANNELS), jnp.float32))
    return lax.map(one_block, jnp.arange(N_TM, dtype=jnp.int32))
```

```python
import functools
import math

import jax
import jax.numpy as jnp
import numpy as np
from jax import lax
from jax.experimental import pallas as pl
from jax.experimental.pallas import tpu as pltpu
from jax.sharding import PartitionSpec as P


CYLINDERS = 4
COL_FEEDS = 256
SECTION_ONE = 128
SECTION_TWO = 128
KEPT = SECTION_TWO // 2
FEED_TILE = 16
VMEM_LIMIT = 67043328
F32 = jnp.float32
BF16 = jnp.bfloat16


def tables(columns, row_count, period, factor):
    turns = np.arange(row_count)[:, None] * np.arange(columns)[None, :] % period
    angles = turns * (2.0 * math.pi / period)
    return ((np.cos(angles) * factor).astype(np.float32), (-np.sin(angles) * factor).astype(np.float32))


def whole_spec(array):
    return pl.BlockSpec(
        array.shape, lambda *_: (0,) * array.ndim, pipeline_mode=pl.Buffered(1)
    )


def channel_kernel(shape, me, *refs):
    del me
    count = sum(shape)
    voltages, small, outs = refs[:count], refs[count : count + 5], refs[count + 5 : -2]
    taps, one, twist_re, twist_im, two = small
    filt, spec = refs[-2:]
    rows = FEED_TILE
    parts = max(shape)

    def fir_of(part):
        blocks, at = [], 0
        for held in shape:
            blocks.append(voltages[at + (part if held > 1 else 0)])
            at += held

        def fir(a, carry):
            lanes = pl.ds(pl.multiple_of(a * SECTION_TWO, SECTION_TWO), SECTION_TWO)
            total = None
            for tap_index, block in enumerate(blocks):
                weight = taps[pl.ds(tap_index, 1), lanes]
                term = weight * block[:, lanes].astype(F32)
                total = term if total is None else total + term
            filt[pl.ds(pl.multiple_of(a * rows, rows), rows), :] = total
            return carry

        lax.fori_loop(0, SECTION_ONE, fir, 0, unroll=8)

    if parts == 1:
        fir_of(0)
    else:
        share = pl.num_programs(0) // parts
        for part in range(parts):
            pl.when(pl.program_id(0) // share == part)(functools.partial(fir_of, part))

    def transform(pair, carry):
        feeds = (2 * pair, 2 * pair + 1)
        framed = jnp.concatenate(
            [filt[pl.ds(f, SECTION_ONE, stride=rows), :].astype(BF16) for f in feeds], axis=1
        )
        first = jnp.dot(one[...], framed, preferred_element_type=F32)
        turned = []
        for i in range(2):
            lanes = slice(i * SECTION_TWO, (i + 1) * SECTION_TWO)
            first_re = first[:SECTION_ONE, lanes]
            first_im = first[SECTION_ONE:, lanes]
            turned_re = first_re * twist_re[...] - first_im * twist_im[...]
            turned_im = first_re * twist_im[...] + first_im * twist_re[...]
            turned.append(
                jnp.concatenate([turned_re.astype(BF16), turned_im.astype(BF16)], axis=1)
            )
        turned = jnp.concatenate(turned, axis=0)
        spectrum = lax.dot_general(
            two[...], turned, (((1,), (1,)), ((), ())), preferred_element_type=F32
        )
        for i, f in enumerate(feeds):
            lanes = slice(i * SECTION_ONE, (i + 1) * SECTION_ONE)
            spec[pl.ds(f, 2 * KEPT, stride=rows), :] = spectrum[:, lanes]
        return carry

    lax.fori_loop(0, rows // 2, transform, 0, unroll=2)
    at = 0
    for out in outs:
        count = out.shape[0]
        piece = spec[at * rows : (at + count) * rows, :]
        out[...] = piece.reshape(count, rows, SECTION_ONE).astype(BF16)
        at += count


def channelize(sources, me, pfb_taps, one, twist_re, twist_im, two, tiles, counts):
    length = SECTION_ONE * SECTION_TWO

    def index(at, skip, limit, i, me):
        return (at, jnp.clip(i + skip, 0, limit), 0)

    specs, operands = [], []
    for held in sources:
        for array, at, skip in held:
            limit = array.shape[1] // FEED_TILE - 1
            specs.append(
                pl.BlockSpec((None, FEED_TILE, length), functools.partial(index, at, skip, limit))
            )
            operands.append(array)
    small = (pfb_taps, one, twist_re, twist_im)
    two_spec = pl.BlockSpec(
        (None,) + two.shape[1:], lambda i, me: (me[0], 0, 0), pipeline_mode=pl.Buffered(1)
    )
    feeds = tiles * FEED_TILE
    return pl.pallas_call(
        functools.partial(channel_kernel, tuple(len(held) for held in sources)),
        grid_spec=pltpu.PrefetchScalarGridSpec(
            num_scalar_prefetch=1,
            grid=(tiles,),
            in_specs=specs + [whole_spec(array) for array in small] + [two_spec],
            out_specs=[
                pl.BlockSpec((count, FEED_TILE, SECTION_ONE), lambda i, me: (0, i, 0))
                for count in counts
            ],
            scratch_shapes=[
                pltpu.VMEM((SECTION_ONE * FEED_TILE, SECTION_TWO), F32),
                pltpu.VMEM((2 * KEPT * FEED_TILE, SECTION_ONE), F32),
            ],
        ),
        out_shape=[jax.ShapeDtypeStruct((count, feeds, SECTION_ONE), BF16) for count in counts],
        compiler_params=pltpu.CompilerParams(
            dimension_semantics=("arbitrary",), vmem_limit_bytes=VMEM_LIMIT
        ),
        cost_estimate=pl.CostEstimate(
            flops=4 * feeds * 256 * 128 * 128,
            bytes_accessed=feeds * length * 2 * 5,
            transcendentals=0,
        ),
    )(me, *operands, *small, two)


def copy_kernel(source, out):
    out[...] = source[...]


def block_of(voltages, at, first, feeds):
    length = voltages.shape[2]
    rows = min(32, feeds)
    skip = first // rows
    return pl.pallas_call(
        copy_kernel,
        grid=(feeds // rows,),
        in_specs=[pl.BlockSpec((1, rows, length), lambda i: (at, i + skip, 0))],
        out_specs=pl.BlockSpec((1, rows, length), lambda i: (0, i, 0)),
        out_shape=jax.ShapeDtypeStruct((1, feeds, length), BF16),
        compiler_params=pltpu.CompilerParams(
            dimension_semantics=("arbitrary",), vmem_limit_bytes=VMEM_LIMIT
        ),
        cost_estimate=pl.CostEstimate(
            flops=0, bytes_accessed=4 * feeds * length, transcendentals=0
        ),
    )(voltages)


def beam_kernel(peers, parts, has_before, *refs):
    count = peers * parts
    arrived, table, out = refs[:count], refs[count], refs[-1]
    before = refs[count + 1] if has_before else None
    slots, lanes = table.shape[0], arrived[0].shape[2]
    for i in range(arrived[0].shape[0] // 2):
        real = jnp.concatenate([a[2 * i] for a in arrived], axis=0)
        imag = jnp.concatenate([a[2 * i + 1] for a in arrived], axis=0)
        data = jnp.concatenate(
            [jnp.concatenate([real, imag], axis=1), jnp.concatenate([-imag, real], axis=1)],
            axis=0,
        )
        at = slice(i * lanes, (i + 1) * lanes)
        step = 512
        for row in range(0, slots, step):
            beam = jnp.dot(table[row : row + step, :], data, preferred_element_type=F32)
            power = beam[:, :lanes] * beam[:, :lanes] + beam[:, lanes:] * beam[:, lanes:]
            if before is not None:
                power = power + before[row : row + step, at]
            out[row : row + step, at] = power


def form_beams(arrived, table, before, channels, first):
    peers, parts = len(arrived), len(arrived[0])
    rows, _, lanes = arrived[0][0].shape
    slots = table.shape[0]
    width = min(2, rows // 2)
    offset = first // width
    out_spec = pl.BlockSpec((slots, width * lanes), lambda i: (0, i + offset))
    operands = [piece for held in arrived for piece in held]
    in_specs = [
        pl.BlockSpec((2 * width, piece.shape[1], lanes), lambda i: (i, 0, 0)) for piece in operands
    ]
    in_specs.append(whole_spec(table))
    operands.append(table)
    aliases = {}
    if before is not None:
        in_specs.append(out_spec)
        operands.append(before)
        aliases = {len(operands) - 1: 0}
    steps = rows // (2 * width)
    return pl.pallas_call(
        functools.partial(beam_kernel, peers, parts, before is not None),
        grid=(steps,),
        in_specs=in_specs,
        out_specs=out_spec,
        out_shape=jax.ShapeDtypeStruct((slots, channels), F32),
        input_output_aliases=aliases,
        compiler_params=pltpu.CompilerParams(
            dimension_semantics=("arbitrary",), vmem_limit_bytes=24 << 20
        ),
        cost_estimate=pl.CostEstimate(
            flops=8 * slots * slots * steps * width * lanes,
            bytes_accessed=8 * slots * steps * width * lanes + 4 * slots * slots,
            transcendentals=0,
        ),
    )(*operands)


def table_kernel(feeds, me, feed_of_slot, waves, out):
    rows = out.shape[0]
    slots = feed_of_slot.shape[0]
    lanes = waves.shape[1]
    shift = COL_FEEDS.bit_length() - 1
    row = pl.program_id(0) * rows + lax.broadcasted_iota(jnp.int32, (rows, lanes), 0)
    p = row & (COL_FEEDS - 1)
    m = row >> shift
    cosine = jnp.broadcast_to(waves[0:1, :], (rows, lanes))
    sine = jnp.broadcast_to(waves[1:2, :], (rows, lanes))
    slot_index = lax.broadcasted_iota(jnp.int32, (slots, lanes), 0)
    lane = lax.broadcasted_iota(jnp.int32, (1, lanes), 1)
    for at in range(0, slots, lanes):
        place = at + lane
        feed = ((place // feeds) ^ me[0]) * feeds + place % feeds
        match = feed_of_slot[...] == feed
        slot = jnp.sum(jnp.where(match, slot_index, 0), axis=0, keepdims=True)
        slot = jnp.broadcast_to(slot, (rows, lanes))
        cylinder = slot >> shift
        turn = p * (slot & (COL_FEEDS - 1)) + m * cylinder * (COL_FEEDS // CYLINDERS)
        turn = turn & (COL_FEEDS - 1)
        index = turn & (lanes - 1)
        real = jnp.take_along_axis(cosine, index, axis=1)
        imag = jnp.take_along_axis(sine, index, axis=1)
        flip = turn >= lanes
        out[:, at : at + lanes] = jnp.where(flip, -real, real).astype(BF16)
        out[:, slots + at : slots + at + lanes] = jnp.where(flip, -imag, imag).astype(BF16)


def beam_table(feed_of_slot, me, feeds):
    slots = CYLINDERS * COL_FEEDS
    half = COL_FEEDS // 2
    factor = 1.0 / math.sqrt(COL_FEEDS) / math.sqrt(CYLINDERS)
    angles = np.arange(half) * (2.0 * math.pi / COL_FEEDS)
    waves = np.zeros((8, half), np.float32)
    waves[0] = np.cos(angles) * factor
    waves[1] = -np.sin(angles) * factor
    rows = 256
    column = feed_of_slot.reshape(slots, 1)
    return pl.pallas_call(
        functools.partial(table_kernel, feeds),
        grid_spec=pltpu.PrefetchScalarGridSpec(
            num_scalar_prefetch=1,
            grid=(slots // rows,),
            in_specs=[whole_spec(column), whole_spec(waves)],
            out_specs=pl.BlockSpec((rows, 2 * slots), lambda i, me: (i, 0)),
        ),
        out_shape=jax.ShapeDtypeStruct((slots, 2 * slots), BF16),
        compiler_params=pltpu.CompilerParams(
            dimension_semantics=("arbitrary",), vmem_limit_bytes=24 << 20
        ),
        cost_estimate=pl.CostEstimate(
            flops=40 * slots * slots, bytes_accessed=4 * slots * slots, transcendentals=0
        ),
    )(me, column, jnp.asarray(waves))


def on_device(voltages, pfb_taps, feed_of_slot):
    spectra_here = voltages.shape[0]
    feeds_here = voltages.shape[1]
    times = lax.axis_size("tm")
    peers = lax.axis_size("feed")
    owned = KEPT // peers
    half = feeds_here // 2
    pairs = [(i + 1, i) for i in range(times - 1)]
    halo = []
    for i in range(spectra_here):
        held = []
        spans = [(0, half), (half, half)] if i == 0 else [(0, feeds_here)]
        for first, count in spans:
            block = block_of(voltages, i, first, count)
            held.append((lax.ppermute(block, "tm", pairs), 0, -first // FEED_TILE))
        halo.append(held)
    me = lax.axis_index("feed").astype(jnp.int32).reshape(1)
    one = jnp.asarray(np.concatenate(tables(SECTION_ONE, SECTION_ONE, SECTION_ONE, 1.0))).astype(BF16)
    factor = 1.0 / math.sqrt(SECTION_ONE * SECTION_TWO)
    twist_re, twist_im = tables(SECTION_TWO, SECTION_ONE, SECTION_ONE * SECTION_TWO, factor)
    two_re, two_im = tables(SECTION_TWO, KEPT, SECTION_TWO, 1.0)
    two = np.stack(
        [
            np.concatenate([two_re, -two_im], axis=1),
            np.concatenate([two_im, two_re], axis=1),
        ],
        axis=1,
    ).reshape(peers, 2 * owned, 2 * SECTION_TWO)
    order = np.arange(peers)[:, None] ^ np.arange(peers)[None, :]
    two = two[order].reshape(peers, 2 * KEPT, 2 * SECTION_TWO).astype(BF16)
    table = beam_table(feed_of_slot, me, feeds_here)
    chunks = []
    for s in range(spectra_here):
        spans = [(0, half), (half, half)] if s == 0 else [(0, feeds_here)]
        gathered = [[] for _ in range(peers)]
        for part, (first, count) in enumerate(spans):
            sources = []
            for tap_index in range(pfb_taps.shape[0]):
                at = s + tap_index
                if at < spectra_here:
                    sources.append([(voltages, at, first // FEED_TILE)])
                elif s == 0:
                    sources.append([(halo[0][part][0], 0, 0)])
                else:
                    sources.append(halo[at - spectra_here])
            pieces = channelize(
                sources,
                me,
                pfb_taps,
                one,
                twist_re,
                twist_im,
                two,
                count // FEED_TILE,
                [2 * owned] * peers,
            )
            gathered[0].append(pieces[0])
            for j in reversed(range(1, peers)):
                gathered[j].append(
                    lax.ppermute(pieces[j], "feed", [(i, i ^ j) for i in range(peers)])
                )
        chunks.append(gathered)
    power = None
    for arrived in chunks:
        power = form_beams(arrived, table, power, owned * SECTION_ONE, 0)
    return power[None]


def solution(mesh):
    in_specs = (P("tm", "feed", None), P(), P())
    out_specs = P("tm", None, "feed")

    return jax.shard_map(
        on_device, mesh=mesh, in_specs=in_specs, out_specs=out_specs, check_vma=False
    )
```

```python
import functools
import math

import jax
import jax.numpy as jnp
import numpy as np
from jax import lax
from jax.experimental import pallas as pl
from jax.experimental.pallas import tpu as pltpu
from jax.sharding import PartitionSpec as P


CYLINDERS = 4
COL_FEEDS = 256
SECTION_ONE = 128
SECTION_TWO = 128
KEPT = SECTION_TWO // 2
FEED_TILE = 16
VMEM_LIMIT = 67043328
F32 = jnp.float32
BF16 = jnp.bfloat16


def tables(columns, row_count, period, factor):
    turns = np.arange(row_count)[:, None] * np.arange(columns)[None, :] % period
    angles = turns * (2.0 * math.pi / period)
    return ((np.cos(angles) * factor).astype(np.float32), (-np.sin(angles) * factor).astype(np.float32))


def whole_spec(array):
    return pl.BlockSpec(
        array.shape, lambda *_: (0,) * array.ndim, pipeline_mode=pl.Buffered(1)
    )


def channel_kernel(me, v0, v1, v2, v3, taps, one, twist_re, twist_im, two, *rest):
    del me
    outs, (filt, spec) = rest[:-2], rest[-2:]
    rows = FEED_TILE
    for a in range(SECTION_ONE):
        lanes = slice(a * SECTION_TWO, (a + 1) * SECTION_TWO)
        total = None
        for tap_index, block in enumerate((v0, v1, v2, v3)):
            term = taps[tap_index : tap_index + 1, lanes] * block[:, lanes].astype(F32)
            total = term if total is None else total + term
        filt[a * rows : (a + 1) * rows, :] = total

    def transform(pair, carry):
        feeds = (2 * pair, 2 * pair + 1)
        framed = jnp.concatenate(
            [filt[pl.ds(f, SECTION_ONE, stride=rows), :].astype(BF16) for f in feeds], axis=1
        )
        first = jnp.dot(one[...], framed, preferred_element_type=F32)
        turned = []
        for i in range(2):
            lanes = slice(i * SECTION_TWO, (i + 1) * SECTION_TWO)
            first_re = first[:SECTION_ONE, lanes]
            first_im = first[SECTION_ONE:, lanes]
            turned_re = first_re * twist_re[...] - first_im * twist_im[...]
            turned_im = first_re * twist_im[...] + first_im * twist_re[...]
            turned.append(
                jnp.concatenate([turned_re.astype(BF16), turned_im.astype(BF16)], axis=1)
            )
        turned = jnp.concatenate(turned, axis=0)
        spectrum = lax.dot_general(
            two[...], turned, (((1,), (1,)), ((), ())), preferred_element_type=F32
        )
        for i, f in enumerate(feeds):
            lanes = slice(i * SECTION_ONE, (i + 1) * SECTION_ONE)
            spec[pl.ds(f, 2 * KEPT, stride=rows), :] = spectrum[:, lanes]
        return carry

    lax.fori_loop(0, rows // 2, transform, 0, unroll=8)
    at = 0
    for out in outs:
        count = out.shape[0]
        piece = spec[at * rows : (at + count) * rows, :]
        out[...] = piece.reshape(count, rows, SECTION_ONE).astype(BF16)
        at += count


def channelize(sources, me, pfb_taps, one, twist_re, twist_im, two, tiles, counts):
    length = SECTION_ONE * SECTION_TWO
    specs = [
        pl.BlockSpec(
            (None, FEED_TILE, length),
            functools.partial(lambda at, skip, i, me: (at, i + skip, 0), at, skip),
        )
        for _, at, skip in sources
    ]
    operands = [array for array, _, _ in sources]
    small = (pfb_taps, one, twist_re, twist_im)
    two_spec = pl.BlockSpec(
        (None,) + two.shape[1:], lambda i, me: (me[0], 0, 0), pipeline_mode=pl.Buffered(1)
    )
    feeds = tiles * FEED_TILE
    return pl.pallas_call(
        channel_kernel,
        grid_spec=pltpu.PrefetchScalarGridSpec(
            num_scalar_prefetch=1,
            grid=(tiles,),
            in_specs=specs + [whole_spec(array) for array in small] + [two_spec],
            out_specs=[
                pl.BlockSpec((count, FEED_TILE, SECTION_ONE), lambda i, me: (0, i, 0))
                for count in counts
            ],
            scratch_shapes=[
                pltpu.VMEM((SECTION_ONE * FEED_TILE, SECTION_TWO), F32),
                pltpu.VMEM((2 * KEPT * FEED_TILE, SECTION_ONE), F32),
            ],
        ),
        out_shape=[jax.ShapeDtypeStruct((count, feeds, SECTION_ONE), BF16) for count in counts],
        compiler_params=pltpu.CompilerParams(
            dimension_semantics=("arbitrary",), vmem_limit_bytes=VMEM_LIMIT
        ),
        cost_estimate=pl.CostEstimate(
            flops=4 * feeds * 256 * 128 * 128,
            bytes_accessed=feeds * length * 2 * 5,
            transcendentals=0,
        ),
    )(me, *operands, *small, two)


def copy_kernel(source, out):
    out[...] = source[...]


def block_of(voltages, at, first, feeds):
    length = voltages.shape[2]
    rows = feeds // 2 if feeds > FEED_TILE else feeds
    skip = first // rows
    return pl.pallas_call(
        copy_kernel,
        grid=(feeds // rows,),
        in_specs=[pl.BlockSpec((1, rows, length), lambda i: (at, i + skip, 0))],
        out_specs=pl.BlockSpec((1, rows, length), lambda i: (0, i, 0)),
        out_shape=jax.ShapeDtypeStruct((1, feeds, length), BF16),
        compiler_params=pltpu.CompilerParams(
            dimension_semantics=("arbitrary",), vmem_limit_bytes=VMEM_LIMIT
        ),
        cost_estimate=pl.CostEstimate(
            flops=0, bytes_accessed=4 * feeds * length, transcendentals=0
        ),
    )(voltages)


def beam_kernel(peers, parts, has_before, *refs):
    count = peers * parts
    arrived, table, out = refs[:count], refs[count], refs[-1]
    before = refs[count + 1] if has_before else None
    slots, lanes = table.shape[0], arrived[0].shape[2]
    for i in range(arrived[0].shape[0] // 2):
        real = jnp.concatenate([a[2 * i] for a in arrived], axis=0)
        imag = jnp.concatenate([a[2 * i + 1] for a in arrived], axis=0)
        data = jnp.concatenate(
            [jnp.concatenate([real, imag], axis=1), jnp.concatenate([-imag, real], axis=1)],
            axis=0,
        )
        at = slice(i * lanes, (i + 1) * lanes)
        step = 512
        for row in range(0, slots, step):
            beam = jnp.dot(table[row : row + step, :], data, preferred_element_type=F32)
            power = beam[:, :lanes] * beam[:, :lanes] + beam[:, lanes:] * beam[:, lanes:]
            if before is not None:
                power = power + before[row : row + step, at]
            out[row : row + step, at] = power


def form_beams(arrived, table, before, channels, first):
    peers, parts = len(arrived), len(arrived[0])
    rows, _, lanes = arrived[0][0].shape
    slots = table.shape[0]
    width = min(2, rows // 2)
    offset = first // width
    out_spec = pl.BlockSpec((slots, width * lanes), lambda i: (0, i + offset))
    operands = [piece for held in arrived for piece in held]
    in_specs = [
        pl.BlockSpec((2 * width, piece.shape[1], lanes), lambda i: (i, 0, 0)) for piece in operands
    ]
    in_specs.append(whole_spec(table))
    operands.append(table)
    aliases = {}
    if before is not None:
        in_specs.append(out_spec)
        operands.append(before)
        aliases = {len(operands) - 1: 0}
    steps = rows // (2 * width)
    return pl.pallas_call(
        functools.partial(beam_kernel, peers, parts, before is not None),
        grid=(steps,),
        in_specs=in_specs,
        out_specs=out_spec,
        out_shape=jax.ShapeDtypeStruct((slots, channels), F32),
        input_output_aliases=aliases,
        compiler_params=pltpu.CompilerParams(
            dimension_semantics=("arbitrary",), vmem_limit_bytes=24 << 20
        ),
        cost_estimate=pl.CostEstimate(
            flops=8 * slots * slots * steps * width * lanes,
            bytes_accessed=8 * slots * steps * width * lanes + 4 * slots * slots,
            transcendentals=0,
        ),
    )(*operands)


def table_kernel(feeds, me, feed_of_slot, waves, out, found):
    rows = out.shape[0]
    slots = feed_of_slot.shape[0]
    lanes = waves.shape[1]
    shift = COL_FEEDS.bit_length() - 1
    row = pl.program_id(0) * rows + lax.broadcasted_iota(jnp.int32, (rows, lanes), 0)
    p = row & (COL_FEEDS - 1)
    m = row >> shift
    cosine = jnp.broadcast_to(waves[0:1, :], (rows, lanes))
    sine = jnp.broadcast_to(waves[1:2, :], (rows, lanes))

    @pl.when(pl.program_id(0) == 0)
    def _():
        slot_index = lax.broadcasted_iota(jnp.int32, (slots, lanes), 0)
        lane = lax.broadcasted_iota(jnp.int32, (1, lanes), 1)
        held = jnp.broadcast_to(feed_of_slot[...], (slots, lanes))
        for at in range(0, slots, lanes):
            place = at + lane
            feed = ((place // feeds) ^ me[0]) * feeds + place % feeds
            slot = jnp.sum(jnp.where(held == feed, slot_index, 0), axis=0, keepdims=True)
            found[:, at : at + lanes] = jnp.broadcast_to(slot, (8, lanes))

    for at in range(0, slots, lanes):
        slot = jnp.broadcast_to(found[0:1, at : at + lanes], (rows, lanes))
        cylinder = slot >> shift
        turn = p * (slot & (COL_FEEDS - 1)) + m * cylinder * (COL_FEEDS // CYLINDERS)
        turn = turn & (COL_FEEDS - 1)
        index = turn & (lanes - 1)
        real = jnp.take_along_axis(cosine, index, axis=1)
        imag = jnp.take_along_axis(sine, index, axis=1)
        flip = turn >= lanes
        out[:, at : at + lanes] = jnp.where(flip, -real, real).astype(BF16)
        out[:, slots + at : slots + at + lanes] = jnp.where(flip, -imag, imag).astype(BF16)


def beam_table(feed_of_slot, me, feeds):
    slots = CYLINDERS * COL_FEEDS
    half = COL_FEEDS // 2
    factor = 1.0 / math.sqrt(COL_FEEDS) / math.sqrt(CYLINDERS)
    angles = np.arange(half) * (2.0 * math.pi / COL_FEEDS)
    waves = np.zeros((8, half), np.float32)
    waves[0] = np.cos(angles) * factor
    waves[1] = -np.sin(angles) * factor
    rows = 256
    column = feed_of_slot.reshape(slots, 1)
    return pl.pallas_call(
        functools.partial(table_kernel, feeds),
        grid_spec=pltpu.PrefetchScalarGridSpec(
            num_scalar_prefetch=1,
            grid=(slots // rows,),
            in_specs=[whole_spec(column), whole_spec(waves)],
            out_specs=pl.BlockSpec((rows, 2 * slots), lambda i, me: (i, 0)),
            scratch_shapes=[pltpu.VMEM((8, slots), jnp.int32)],
        ),
        out_shape=jax.ShapeDtypeStruct((slots, 2 * slots), BF16),
        compiler_params=pltpu.CompilerParams(
            dimension_semantics=("arbitrary",), vmem_limit_bytes=24 << 20
        ),
        cost_estimate=pl.CostEstimate(
            flops=40 * slots * slots, bytes_accessed=4 * slots * slots, transcendentals=0
        ),
    )(me, column, jnp.asarray(waves))


def on_device(voltages, pfb_taps, feed_of_slot):
    spectra_here = voltages.shape[0]
    feeds_here = voltages.shape[1]
    times = lax.axis_size("tm")
    peers = lax.axis_size("feed")
    owned = KEPT // peers
    lead = max(1, 3 * feeds_here // (8 * FEED_TILE)) * FEED_TILE
    pairs = [(i + 1, i) for i in range(times - 1)]
    early = lax.ppermute(block_of(voltages, 0, 0, lead), "tm", pairs)
    following = lax.ppermute(voltages, "tm", pairs)
    me = lax.axis_index("feed").astype(jnp.int32).reshape(1)
    one = jnp.asarray(np.concatenate(tables(SECTION_ONE, SECTION_ONE, SECTION_ONE, 1.0))).astype(BF16)
    factor = 1.0 / math.sqrt(SECTION_ONE * SECTION_TWO)
    twist_re, twist_im = tables(SECTION_TWO, SECTION_ONE, SECTION_ONE * SECTION_TWO, factor)
    two_re, two_im = tables(SECTION_TWO, KEPT, SECTION_TWO, 1.0)
    two = np.stack(
        [
            np.concatenate([two_re, -two_im], axis=1),
            np.concatenate([two_im, two_re], axis=1),
        ],
        axis=1,
    ).reshape(peers, 2 * owned, 2 * SECTION_TWO)
    order = np.arange(peers)[:, None] ^ np.arange(peers)[None, :]
    two = two[order]

    def split_table(shares):
        held, at = [], 0
        for wide in shares:
            held.append(two[:, :, 2 * at : 2 * (at + wide)].reshape(peers, -1, 2 * SECTION_TWO))
            at += wide
        return jnp.asarray(np.concatenate(held, axis=1)).astype(BF16)

    table = beam_table(feed_of_slot, me, feeds_here)
    first_spans = [(0, lead), (lead, feeds_here - lead)]
    last_share = max(1, owned // 2)
    chunks = []
    for s in range(spectra_here):
        spans = first_spans if s == 0 else [(0, feeds_here)]
        shares = [owned - last_share, last_share] if s == spectra_here - 1 else [owned]
        gathered = [[[] for _ in range(peers)] for _ in shares]
        for first, count in spans:
            skip = first // FEED_TILE
            sources = []
            for tap_index in range(pfb_taps.shape[0]):
                at = s + tap_index
                if at < spectra_here:
                    sources.append((voltages, at, skip))
                elif s == 0 and first < lead:
                    sources.append((early, 0, skip))
                else:
                    sources.append((following, at - spectra_here, skip))
            pieces = channelize(
                sources,
                me,
                pfb_taps,
                one,
                twist_re,
                twist_im,
                split_table(shares),
                count // FEED_TILE,
                [2 * wide for wide in shares for _ in range(peers)],
            )
            for split in range(len(shares)):
                mine = pieces[split * peers : (split + 1) * peers]
                gathered[split][0].append(mine[0])
                for j in reversed(range(1, peers)):
                    gathered[split][j].append(
                        lax.ppermute(mine[j], "feed", [(i, i ^ j) for i in range(peers)])
                    )
        for split, held in enumerate(gathered):
            chunks.append((held, sum(shares[:split])))
    power = None
    for arrived, first in chunks:
        power = form_beams(arrived, table, power, owned * SECTION_ONE, first)
    return power[None]


def solution(mesh):
    in_specs = (P("tm", "feed", None), P(), P())
    out_specs = P("tm", None, "feed")

    return jax.shard_map(
        on_device, mesh=mesh, in_specs=in_specs, out_specs=out_specs, check_vma=False
    )
```

```python
import functools
import math

import jax
import jax.numpy as jnp
import numpy as np
from jax import lax
from jax.experimental import pallas as pl
from jax.experimental.pallas import tpu as pltpu
from jax.sharding import PartitionSpec as P


CYLINDERS = 4
COL_FEEDS = 256
SECTION_ONE = 128
SECTION_TWO = 128
KEPT = SECTION_TWO // 2
FEED_TILE = 16
VMEM_LIMIT = 67043328
F32 = jnp.float32
BF16 = jnp.bfloat16


def tables(columns, row_count, period, factor):
    turns = np.arange(row_count)[:, None] * np.arange(columns)[None, :] % period
    angles = turns * (2.0 * math.pi / period)
    return ((np.cos(angles) * factor).astype(np.float32), (-np.sin(angles) * factor).astype(np.float32))


def whole_spec(array):
    return pl.BlockSpec(
        array.shape, lambda *_: (0,) * array.ndim, pipeline_mode=pl.Buffered(1)
    )


def channel_kernel(me, v0, v1, v2, v3, taps, one, twist_re, twist_im, two, *rest):
    del me
    outs, (filt, spec) = rest[:-2], rest[-2:]
    rows = FEED_TILE
    for a in range(SECTION_ONE):
        lanes = slice(a * SECTION_TWO, (a + 1) * SECTION_TWO)
        total = None
        for tap_index, block in enumerate((v0, v1, v2, v3)):
            term = taps[tap_index : tap_index + 1, lanes] * block[:, lanes].astype(F32)
            total = term if total is None else total + term
        filt[a * rows : (a + 1) * rows, :] = total

    def transform(pair, carry):
        feeds = (2 * pair, 2 * pair + 1)
        framed = jnp.concatenate(
            [filt[pl.ds(f, SECTION_ONE, stride=rows), :].astype(BF16) for f in feeds], axis=1
        )
        first = jnp.dot(one[...], framed, preferred_element_type=F32)
        turned = []
        for i in range(2):
            lanes = slice(i * SECTION_TWO, (i + 1) * SECTION_TWO)
            first_re = first[:SECTION_ONE, lanes]
            first_im = first[SECTION_ONE:, lanes]
            turned_re = first_re * twist_re[...] - first_im * twist_im[...]
            turned_im = first_re * twist_im[...] + first_im * twist_re[...]
            turned.append(
                jnp.concatenate([turned_re.astype(BF16), turned_im.astype(BF16)], axis=1)
            )
        turned = jnp.concatenate(turned, axis=0)
        spectrum = lax.dot_general(
            two[...], turned, (((1,), (1,)), ((), ())), preferred_element_type=F32
        )
        for i, f in enumerate(feeds):
            lanes = slice(i * SECTION_ONE, (i + 1) * SECTION_ONE)
            spec[pl.ds(f, 2 * KEPT, stride=rows), :] = spectrum[:, lanes]
        return carry

    lax.fori_loop(0, rows // 2, transform, 0, unroll=8)
    at = 0
    for out in outs:
        count = out.shape[0]
        piece = spec[at * rows : (at + count) * rows, :]
        out[...] = piece.reshape(count, rows, SECTION_ONE).astype(BF16)
        at += count


def channelize(sources, me, pfb_taps, one, twist_re, twist_im, two, tiles, counts):
    length = SECTION_ONE * SECTION_TWO
    specs = [
        pl.BlockSpec(
            (None, FEED_TILE, length),
            functools.partial(lambda at, skip, i, me: (at, i + skip, 0), at, skip),
        )
        for _, at, skip in sources
    ]
    operands = [array for array, _, _ in sources]
    small = (pfb_taps, one, twist_re, twist_im)
    two_spec = pl.BlockSpec(
        (None,) + two.shape[1:], lambda i, me: (me[0], 0, 0), pipeline_mode=pl.Buffered(1)
    )
    feeds = tiles * FEED_TILE
    return pl.pallas_call(
        channel_kernel,
        grid_spec=pltpu.PrefetchScalarGridSpec(
            num_scalar_prefetch=1,
            grid=(tiles,),
            in_specs=specs + [whole_spec(array) for array in small] + [two_spec],
            out_specs=[
                pl.BlockSpec((count, FEED_TILE, SECTION_ONE), lambda i, me: (0, i, 0))
                for count in counts
            ],
            scratch_shapes=[
                pltpu.VMEM((SECTION_ONE * FEED_TILE, SECTION_TWO), F32),
                pltpu.VMEM((2 * KEPT * FEED_TILE, SECTION_ONE), F32),
            ],
        ),
        out_shape=[jax.ShapeDtypeStruct((count, feeds, SECTION_ONE), BF16) for count in counts],
        compiler_params=pltpu.CompilerParams(
            dimension_semantics=("arbitrary",), vmem_limit_bytes=VMEM_LIMIT
        ),
        cost_estimate=pl.CostEstimate(
            flops=4 * feeds * 256 * 128 * 128,
            bytes_accessed=feeds * length * 2 * 5,
            transcendentals=0,
        ),
    )(me, *operands, *small, two)


def copy_kernel(source, out):
    out[...] = source[...]


def block_of(voltages, at, first, feeds):
    length = voltages.shape[2]
    rows = feeds // 2 if feeds > FEED_TILE else feeds
    skip = first // rows
    return pl.pallas_call(
        copy_kernel,
        grid=(feeds // rows,),
        in_specs=[pl.BlockSpec((1, rows, length), lambda i: (at, i + skip, 0))],
        out_specs=pl.BlockSpec((1, rows, length), lambda i: (0, i, 0)),
        out_shape=jax.ShapeDtypeStruct((1, feeds, length), BF16),
        compiler_params=pltpu.CompilerParams(
            dimension_semantics=("arbitrary",), vmem_limit_bytes=VMEM_LIMIT
        ),
        cost_estimate=pl.CostEstimate(
            flops=0, bytes_accessed=4 * feeds * length, transcendentals=0
        ),
    )(voltages)


def beam_kernel(peers, parts, has_before, *refs):
    count = peers * parts
    arrived, table, out = refs[:count], refs[count], refs[-1]
    before = refs[count + 1] if has_before else None
    lanes = arrived[0].shape[2]
    half, rows = COL_FEEDS // 2, COL_FEEDS // 2 + 8
    line = lax.broadcasted_iota(jnp.int32, (8, lanes), 0)
    mirror = (8 - line) & 7
    for i in range(arrived[0].shape[0] // 2):
        data = jnp.concatenate(
            [
                jnp.concatenate([a[2 * i + e] for a in arrived], axis=0)
                for e in range(2)
            ],
            axis=1,
        )
        at = slice(i * lanes, (i + 1) * lanes)

        def put(first, power):
            to = slice(first, first + half)
            if before is not None:
                power = power + before[to, at]
            out[to, at] = power

        for m in range(CYLINDERS):
            both = jnp.dot(
                table[2 * m * rows : 2 * (m + 1) * rows, :], data, preferred_element_type=F32
            )
            cos_re, cos_im = both[:rows, :lanes], both[:rows, lanes:]
            sin_re, sin_im = both[rows:, :lanes], both[rows:, lanes:]
            real = cos_re[:half] - sin_im[:half]
            imag = cos_im[:half] + sin_re[:half]
            put(m * COL_FEEDS, real * real + imag * imag)
            real = cos_re + sin_im
            imag = cos_im - sin_re
            power = real * real + imag * imag
            tiles = [
                jnp.take_along_axis(power[8 * k : 8 * k + 8], mirror, axis=0)
                for k in range(rows // 8)
            ]
            turned = [
                jnp.where(line == 0, tiles[half // 8 - t], tiles[half // 8 - 1 - t])
                for t in range(half // 8)
            ]
            other = (CYLINDERS - m) % CYLINDERS
            put(other * COL_FEEDS + half, jnp.concatenate(turned, axis=0))


def form_beams(arrived, table, before, channels, first):
    peers, parts = len(arrived), len(arrived[0])
    rows, _, lanes = arrived[0][0].shape
    slots = table.shape[1]
    width = min(2, rows // 2)
    offset = first // width
    out_spec = pl.BlockSpec((slots, width * lanes), lambda i: (0, i + offset))
    operands = [piece for held in arrived for piece in held]
    in_specs = [
        pl.BlockSpec((2 * width, piece.shape[1], lanes), lambda i: (i, 0, 0)) for piece in operands
    ]
    in_specs.append(whole_spec(table))
    operands.append(table)
    aliases = {}
    if before is not None:
        in_specs.append(out_spec)
        operands.append(before)
        aliases = {len(operands) - 1: 0}
    steps = rows // (2 * width)
    return pl.pallas_call(
        functools.partial(beam_kernel, peers, parts, before is not None),
        grid=(steps,),
        in_specs=in_specs,
        out_specs=out_spec,
        out_shape=jax.ShapeDtypeStruct((slots, channels), F32),
        input_output_aliases=aliases,
        compiler_params=pltpu.CompilerParams(
            dimension_semantics=("arbitrary",), vmem_limit_bytes=24 << 20
        ),
        cost_estimate=pl.CostEstimate(
            flops=4 * slots * slots * steps * width * lanes,
            bytes_accessed=8 * slots * steps * width * lanes + 4 * slots * slots,
            transcendentals=0,
        ),
    )(*operands)


def table_kernel(feeds, me, feed_of_slot, waves, out, found):
    rows = out.shape[0]
    slots = feed_of_slot.shape[0]
    lanes = waves.shape[1]
    shift = COL_FEEDS.bit_length() - 1
    row = lax.broadcasted_iota(jnp.int32, (rows, lanes), 0)
    m = pl.program_id(0)
    lower = row >= rows // 2
    p = jnp.where(lower, row - rows // 2, row)
    quarter = jnp.where(lower, COL_FEEDS // 4, 0)
    cosine = jnp.broadcast_to(waves[0:1, :], (rows, lanes))

    @pl.when(pl.program_id(0) == 0)
    def _():
        slot_index = lax.broadcasted_iota(jnp.int32, (slots, lanes), 0)
        lane = lax.broadcasted_iota(jnp.int32, (1, lanes), 1)
        held = jnp.broadcast_to(feed_of_slot[...], (slots, lanes))
        for at in range(0, slots, lanes):
            place = at + lane
            feed = ((place // feeds) ^ me[0]) * feeds + place % feeds
            slot = jnp.sum(jnp.where(held == feed, slot_index, 0), axis=0, keepdims=True)
            found[:, at : at + lanes] = jnp.broadcast_to(slot, (8, lanes))

    for at in range(0, slots, lanes):
        slot = jnp.broadcast_to(found[0:1, at : at + lanes], (rows, lanes))
        cylinder = slot >> shift
        turn = p * (slot & (COL_FEEDS - 1)) + m * cylinder * (COL_FEEDS // CYLINDERS)
        turn = (turn + quarter) & (COL_FEEDS - 1)
        value = jnp.take_along_axis(cosine, turn & (lanes - 1), axis=1)
        out[:, at : at + lanes] = jnp.where(turn >= lanes, -value, value).astype(BF16)


def beam_table(feed_of_slot, me, feeds):
    slots = CYLINDERS * COL_FEEDS
    half = COL_FEEDS // 2
    factor = 1.0 / math.sqrt(COL_FEEDS) / math.sqrt(CYLINDERS)
    angles = np.arange(half) * (2.0 * math.pi / COL_FEEDS)
    waves = np.zeros((8, half), np.float32)
    waves[0] = np.cos(angles) * factor
    rows = 2 * (half + 8)
    column = feed_of_slot.reshape(slots, 1)
    return pl.pallas_call(
        functools.partial(table_kernel, feeds),
        grid_spec=pltpu.PrefetchScalarGridSpec(
            num_scalar_prefetch=1,
            grid=(CYLINDERS,),
            in_specs=[whole_spec(column), whole_spec(waves)],
            out_specs=pl.BlockSpec((rows, slots), lambda i, me: (i, 0)),
            scratch_shapes=[pltpu.VMEM((8, slots), jnp.int32)],
        ),
        out_shape=jax.ShapeDtypeStruct((CYLINDERS * rows, slots), BF16),
        compiler_params=pltpu.CompilerParams(
            dimension_semantics=("arbitrary",), vmem_limit_bytes=24 << 20
        ),
        cost_estimate=pl.CostEstimate(
            flops=40 * slots * slots, bytes_accessed=4 * slots * slots, transcendentals=0
        ),
    )(me, column, jnp.asarray(waves))


def on_device(voltages, pfb_taps, feed_of_slot):
    spectra_here = voltages.shape[0]
    feeds_here = voltages.shape[1]
    times = lax.axis_size("tm")
    peers = lax.axis_size("feed")
    owned = KEPT // peers
    lead = max(1, feeds_here // (4 * FEED_TILE)) * FEED_TILE
    pairs = [(i + 1, i) for i in range(times - 1)]
    early = lax.ppermute(block_of(voltages, 0, 0, lead), "tm", pairs)
    following = lax.ppermute(voltages, "tm", pairs)
    me = lax.axis_index("feed").astype(jnp.int32).reshape(1)
    one = jnp.asarray(np.concatenate(tables(SECTION_ONE, SECTION_ONE, SECTION_ONE, 1.0))).astype(BF16)
    factor = 1.0 / math.sqrt(SECTION_ONE * SECTION_TWO)
    twist_re, twist_im = tables(SECTION_TWO, SECTION_ONE, SECTION_ONE * SECTION_TWO, factor)
    two_re, two_im = tables(SECTION_TWO, KEPT, SECTION_TWO, 1.0)
    two = np.stack(
        [
            np.concatenate([two_re, -two_im], axis=1),
            np.concatenate([two_im, two_re], axis=1),
        ],
        axis=1,
    ).reshape(peers, 2 * owned, 2 * SECTION_TWO)
    order = np.arange(peers)[:, None] ^ np.arange(peers)[None, :]
    two = two[order]

    def split_table(shares):
        held, at = [], 0
        for wide in shares:
            held.append(two[:, :, 2 * at : 2 * (at + wide)].reshape(peers, -1, 2 * SECTION_TWO))
            at += wide
        return jnp.asarray(np.concatenate(held, axis=1)).astype(BF16)

    table = beam_table(feed_of_slot, me, feeds_here)
    first_spans = [(0, lead), (lead, feeds_here - lead)]
    last_share = max(1, owned // 2)
    chunks = []
    for s in range(spectra_here):
        spans = first_spans if s == 0 else [(0, feeds_here)]
        shares = [owned - last_share, last_share] if s == spectra_here - 1 else [owned]
        gathered = [[[] for _ in range(peers)] for _ in shares]
        for first, count in spans:
            skip = first // FEED_TILE
            sources = []
            for tap_index in range(pfb_taps.shape[0]):
                at = s + tap_index
                if at < spectra_here:
                    sources.append((voltages, at, skip))
                elif s == 0 and first < lead:
                    sources.append((early, 0, skip))
                else:
                    sources.append((following, at - spectra_here, skip))
            pieces = channelize(
                sources,
                me,
                pfb_taps,
                one,
                twist_re,
                twist_im,
                split_table(shares),
                count // FEED_TILE,
                [2 * wide for wide in shares for _ in range(peers)],
            )
            for split in range(len(shares)):
                mine = pieces[split * peers : (split + 1) * peers]
                gathered[split][0].append(mine[0])
                for j in reversed(range(1, peers)):
                    gathered[split][j].append(
                        lax.ppermute(mine[j], "feed", [(i, i ^ j) for i in range(peers)])
                    )
        for split, held in enumerate(gathered):
            chunks.append((held, sum(shares[:split])))
    power = None
    for arrived, first in chunks:
        power = form_beams(arrived, table, power, owned * SECTION_ONE, first)
    return power[None]


def solution(mesh):
    in_specs = (P("tm", "feed", None), P(), P())
    out_specs = P("tm", None, "feed")

    return jax.shard_map(
        on_device, mesh=mesh, in_specs=in_specs, out_specs=out_specs, check_vma=False
    )
```
